512 devices in a mesh: chan: 32 (over y, z_lo), ctx: 16 (over z_hi, x, core).
Axes of the slice: x: 4, y: 4, z: 16 (z_hi: 2, z_lo: 8; z = z_hi * 8 + z_lo), core: 2. Of those that a mesh axis runs over, the one named last changes fastest.
Arguments:
- inputs: bfloat16 [2048, 8192], P('ctx', 'chan'), may hold values from -6 to 6
- gate: bfloat16 [2048, 8192], P('ctx', 'chan'), may hold values from -200 to 200
- filter_taps: bfloat16 [2048, 8192], P('ctx', 'chan'), may hold values from -4 to 4, as said below
- cotangent: bfloat16 [2048, 8192], P('ctx', 'chan'), may hold values from -6 to 6
Outputs:
- output: bfloat16 [2048, 8192], P('ctx', 'chan')
- gate_grad: bfloat16 [2048, 8192], P('ctx', 'chan')
- input_grad: bfloat16 [2048, 8192], P('ctx', 'chan')
- filter_grad: float32 [2048, 8192], P('ctx', 'chan')
The draws below stay inside these ranges and needn't reach their ends.
Inputs may be any that keep to these rules, and one draw needn't show every extreme that they name: `filter_taps`: each channel's filter taps shrink with the lag at a rate of their own.
All inputs are finite; a program needn't handle non-finite values.
Results may differ from the reference program's by a relative error of at most 0.005.
Values may be sent and summed in bfloat16 or wider, within the bound.
A program may use at most 64 MiB of HBM per device.

```python
import math
import jax
import jax.numpy as jnp
from jax import lax

CH = 8192
TOK_DEV = 128
TOKENS = 2048


def draw_filter_taps(key, part):
    key_rate, key_spot, key_noise = jax.random.split(key, 3)
    lags = jnp.arange(TOKENS, dtype=jnp.float32)[:, None]
    lowest = float(max(2, min(40, TOK_DEV // 4)))
    highest = 16.0 * TOKENS
    spread = jax.random.uniform(key_rate, (1, CH), jnp.float32)
    decay_len = lowest * jnp.exp(spread * jnp.log(highest / lowest))
    spots = jax.random.randint(key_spot, (3,), 1, TOKENS).astype(jnp.float32)
    drops = jnp.sum((lags[:, :, None] >= spots[None, None, :]).astype(jnp.float32), axis=2)
    keeping = jnp.exp(drops * jnp.log(0.6))
    scaling = jnp.sqrt((1.0 - jnp.exp(-2.0 / decay_len)) / (1.0 - jnp.exp(-2.0 * TOKENS / decay_len)))
    noise = jnp.clip(jax.random.normal(key_noise, (TOKENS, CH), jnp.float32), -5.0, 5.0)
    return (noise * jnp.exp(-lags / decay_len) * scaling * keeping).astype(jnp.bfloat16)


def draw_gate(key, part):
    key_col, key_row, key_base = jax.random.split(key, 3)
    channel = jnp.arange(CH, dtype=jnp.float32)[None, :] / CH
    rising = jnp.exp(channel * jnp.log(3.0))
    column = jnp.exp(jax.random.uniform(key_col, (1, CH), jnp.float32) * jnp.log(4.0))
    row_scale = 0.316 * jnp.exp(jax.random.uniform(key_row, (TOKENS, 1), jnp.float32) * jnp.log(10.0))
    base = jnp.clip(jax.random.normal(key_base, (TOKENS, CH), jnp.float32), -4.0, 4.0)
    return (base * rising * column * row_scale).astype(jnp.bfloat16)


def steps_of(own_key, extent, cuts, low, high):
    level = 1.0
    for dim, parts in cuts:
        steps = jax.random.uniform(jax.random.fold_in(jax.random.fold_in(own_key, 6), dim), (parts,), jnp.float32, low / len(cuts), high / len(cuts))
        level = level * jnp.repeat(jnp.exp(steps), extent[dim] // parts).reshape((-1,) + (1,) * (len(extent) - 1 - dim))
    return level


def scatter_about(rng, shape, width, reach, cuts=(), kind=jnp.bfloat16):
    entries = width * jax.random.normal(rng, shape, jnp.float32)
    if cuts:
        entries = entries * steps_of(rng, shape, cuts, -0.22, 0.18)
    return jnp.clip(entries, -reach, reach).astype(kind)


def setup_inputs(seed: int = 0) -> dict:
    streams_of = jax.random.split(jax.random.key(seed), 5)
    inputs = scatter_about(streams_of[0], (TOKENS, CH), 1.0, 6.0, ((0, 16), (1, 32)))
    gate = draw_gate(jax.random.fold_in(streams_of[4], 71), 0)
    filter_taps = draw_filter_taps(jax.random.fold_in(streams_of[4], 71), 0)
    cotangent = scatter_about(streams_of[3], (TOKENS, CH), 1.0, 6.0, ((0, 16), (1, 32)))
    return {"inputs": inputs, "gate": gate, "filter_taps": filter_taps, "cotangent": cotangent}


EPSILON = 1e-06

def causal(signal, kernel):
    length = signal.shape[0]
    size = 2 * length
    joined = jnp.fft.rfft(signal, size, axis=0) * jnp.fft.rfft(kernel, size, axis=0)
    return jnp.fft.irfft(joined, size, axis=0)[:length]

def lagged(earlier, later):
    length = earlier.shape[0]
    size = 2 * length
    joined = jnp.conj(jnp.fft.rfft(earlier, size, axis=0)) * jnp.fft.rfft(later, size, axis=0)
    return jnp.fft.irfft(joined, size, axis=0)[:length]

def reference(inputs, gate, filter_taps, cotangent):
    signal = inputs.astype(jnp.float32)
    taps = filter_taps.astype(jnp.float32)
    gate_wide = gate.astype(jnp.float32)
    upstream = cotangent.astype(jnp.float32)
    convolved = causal(signal, taps).astype(jnp.float32)
    mixed = gate_wide * convolved
    inv_rms = lax.rsqrt(lax.optimization_barrier(jnp.sum(mixed * mixed, axis=1, keepdims=True)) / CH + EPSILON)
    output = (mixed * inv_rms).astype(jnp.bfloat16)
    projection = lax.optimization_barrier(jnp.sum(upstream * mixed, axis=1, keepdims=True))
    d_mixed = inv_rms * upstream - mixed * inv_rms ** 3 * projection / CH
    gate_grad = (d_mixed * convolved).astype(jnp.bfloat16)
    d_inner = (d_mixed * gate_wide).astype(jnp.bfloat16).astype(jnp.float32)
    input_grad = lagged(taps, d_inner).astype(jnp.bfloat16)
    filter_grad = (lagged(signal, d_inner) / math.sqrt(TOKENS)).astype(jnp.float32)
    return (output, gate_grad, input_grad, filter_grad)
```

```python
import functools
import math

import jax
import jax.numpy as jnp
import ml_dtypes
import numpy as np
from jax import lax
from jax.experimental import pallas as pl
from jax.experimental.pallas import tpu as pltpu
from jax.sharding import PartitionSpec as P

EPSILON = 1e-06
MESH = pl.DeviceIdType.MESH
BF16 = jnp.bfloat16
F32 = jnp.float32


def split_table(table):
    head = table.astype(ml_dtypes.bfloat16)
    rest = (table - head.astype(np.float64)).astype(ml_dtypes.bfloat16)
    return head, rest


def dft_tables(n):
    k = np.arange(n)
    t = np.arange(n)
    angles = np.mod(np.outer(t, k), 2 * n) * (math.pi / n)
    alternate = np.where(t % 2 == 0, 1.0, -1.0)
    sines = -np.sin(angles)
    sines[:, 0] = alternate
    fwd = np.concatenate([np.cos(angles), sines], axis=1)
    weights = np.where(k == 0, 1.0, 2.0) / (2 * n)
    inv = np.concatenate(
        [np.cos(angles) * weights[None, :], sines * weights[None, :]], axis=1
    ).T
    return split_table(fwd) + split_table(inv)


def kernel(
    nb, nchan,
    x_ref, g_ref, h_ref, c_ref, fhi_ref, flo_ref, ihi_ref, ilo_ref,
    out_ref, gg_ref, ig_ref, fg_ref,
    s1, r1, s2, r2, s3, r3, s4, r4, stats,
    xre, xim, kre, kre2, kim, vre, vim, qre, qim,
    send_sems, recv_sems, stat_send, stat_recv,
):
    me = lax.axis_index("ctx")
    mc = lax.axis_index("chan")
    n, local_chan = x_ref.shape
    cb = local_chan // nb
    rows = nb * cb
    channels = local_chan * nchan

    barrier = pltpu.get_barrier_semaphore()

    def greet_ctx(k, _):
        pl.semaphore_signal(
            barrier, inc=1, device_id={"ctx": lax.rem(me + k, nb)}, device_id_type=MESH
        )
        return 0

    def greet_chan(k, _):
        pl.semaphore_signal(
            barrier, inc=1, device_id={"chan": lax.rem(mc + k, nchan)}, device_id_type=MESH
        )
        return 0

    lax.fori_loop(1, nb, greet_ctx, 0)
    lax.fori_loop(1, nchan, greet_chan, 0)

    def turned(ref):
        return ref[...].astype(F32).T

    s1[:, 0] = turned(x_ref).astype(BF16).reshape(nb, cb, n)
    s1[:, 1] = turned(h_ref).astype(BF16).reshape(nb, cb, n)
    pl.semaphore_wait(barrier, nb + nchan - 2)

    def exchange(phase, src, dst, k):
        return pltpu.make_async_remote_copy(
            src_ref=src.at[lax.rem(me + k, nb)],
            dst_ref=dst.at[me],
            send_sem=send_sems.at[phase, k],
            recv_sem=recv_sems.at[phase, k],
            device_id={"ctx": lax.rem(me + k, nb)},
            device_id_type=MESH,
        )

    def start_exchange(phase, src, dst):
        def step(k, _):
            exchange(phase, src, dst, k).start()
            return 0

        lax.fori_loop(1, nb, step, 0)
        dst[me] = src[me]

    def arrived(phase, src, dst, k):
        return pltpu.make_async_remote_copy(
            src_ref=src.at[lax.rem(me + nb - k, nb)],
            dst_ref=dst.at[lax.rem(me + nb - k, nb)],
            send_sem=send_sems.at[phase, k],
            recv_sem=recv_sems.at[phase, k],
            device_id={"ctx": lax.rem(me + nb - k, nb)},
            device_id_type=MESH,
        )

    def finish_exchange(phase, src, dst):
        def step(k, _):
            arrived(phase, src, dst, k).wait_recv()
            return 0

        lax.fori_loop(1, nb, step, 0)

    def sent(phase, src, dst):
        def step(k, _):
            exchange(phase, src, dst, k).wait_send()
            return 0

        lax.fori_loop(1, nb, step, 0)

    lane = lax.broadcasted_iota(jnp.int32, (1, 1, n), 2)
    alternate = jnp.where(lax.rem(lane, 2) == 0, 1.0, -1.0).astype(F32)
    first = lane == 0

    def spectrum(block):
        wide = jnp.dot(block, fhi_ref[...], preferred_element_type=F32) + jnp.dot(
            block, flo_ref[...], preferred_element_type=F32
        )
        return wide[:, :n].reshape(nb, cb, n), wide[:, n:].reshape(nb, cb, n)

    def inverse():
        def half(part, lo, hi):
            head = part.astype(BF16)
            rest = (part - head.astype(F32)).astype(BF16)
            return (
                jnp.dot(head, ihi_ref[lo:hi, :], preferred_element_type=F32)
                + jnp.dot(head, ilo_ref[lo:hi, :], preferred_element_type=F32)
                + jnp.dot(rest, ihi_ref[lo:hi, :], preferred_element_type=F32)
            )

        return half(qre[...].reshape(rows, n), 0, n) + half(qim[...].reshape(rows, n), n, 2 * n)

    def set_kernel(re, im):
        kre[...] = re
        kre2[...] = jnp.where(first, im, re)
        kim[...] = jnp.where(first, 0.0, im)

    def correlate():
        for d in range(nb):
            re, im = vre[d:], vim[d:]
            a, a2, b = kre[d : d + 1], kre2[d : d + 1], kim[d : d + 1]
            new_re = a * re + b * im
            new_im = a2 * im - b * re
            if d == 0:
                qre[...] = new_re
                qim[...] = new_im
            else:
                qre[: nb - d] += new_re
                qim[: nb - d] += new_im

    start_exchange(0, s1, r1)
    gate = turned(g_ref)
    upstream = turned(c_ref)
    finish_exchange(0, s1, r1)

    x_re, x_im = spectrum(r1[:, 0].reshape(rows, n))
    xre[...] = x_re
    xim[...] = x_im
    h_re, h_im = spectrum(r1[:, 1].reshape(rows, n))
    zero = jnp.zeros((1, cb, n), F32)
    set_kernel(
        h_re + alternate * jnp.concatenate([zero, h_re[:-1]], axis=0),
        h_im + alternate * jnp.concatenate([zero, h_im[:-1]], axis=0),
    )
    for d in range(nb):
        re, im = xre[: nb - d], xim[: nb - d]
        a, a2, b = kre[d : d + 1], kre2[d : d + 1], kim[d : d + 1]
        new_re = a * re - b * im
        new_im = b * re + a2 * im
        if d == 0:
            qre[...] = new_re
            qim[...] = new_im
        else:
            qre[d:] += new_re
            qim[d:] += new_im
    s2[...] = inverse().astype(BF16).reshape(nb, cb, n)
    start_exchange(1, s2, r2)
    finish_exchange(1, s2, r2)

    convolved = r2[...].reshape(rows, n).astype(F32)
    mixed = gate * convolved
    stats[mc, 0:1, :] = jnp.sum(mixed * mixed, axis=0, keepdims=True)
    stats[mc, 1:2, :] = jnp.sum(upstream * mixed, axis=0, keepdims=True)

    def stat_copy(k):
        return pltpu.make_async_remote_copy(
            src_ref=stats.at[mc],
            dst_ref=stats.at[mc],
            send_sem=stat_send.at[k],
            recv_sem=stat_recv.at[k],
            device_id={"chan": lax.rem(mc + k, nchan)},
            device_id_type=MESH,
        )

    def stat_start(k, _):
        stat_copy(k).start()
        return 0

    def stat_wait(k, _):
        source = lax.rem(mc + nchan - k, nchan)
        pltpu.make_async_remote_copy(
            src_ref=stats.at[source],
            dst_ref=stats.at[source],
            send_sem=stat_send.at[k],
            recv_sem=stat_recv.at[k],
            device_id={"chan": source},
            device_id_type=MESH,
        ).wait_recv()
        return 0

    def stat_sent(k, _):
        stat_copy(k).wait_send()
        return 0

    lax.fori_loop(1, nchan, stat_start, 0)
    lax.fori_loop(1, nchan, stat_wait, 0)
    totals = jnp.sum(stats[...], axis=0)
    inv_rms = lax.rsqrt(totals[0:1] / channels + EPSILON)
    d_mixed = inv_rms * upstream - mixed * (inv_rms**3 * totals[1:2] / channels)
    s3[...] = (d_mixed * gate).astype(BF16).reshape(nb, cb, n)
    start_exchange(2, s3, r3)
    out_ref[...] = (mixed * inv_rms).T.astype(BF16)
    gg_ref[...] = (d_mixed * convolved).T.astype(BF16)
    finish_exchange(2, s3, r3)

    d_re, d_im = spectrum(r3[...].reshape(rows, n))
    vre[...] = d_re
    vim[...] = d_im
    correlate()
    s4[:, 0] = inverse().astype(BF16).reshape(nb, cb, n)
    set_kernel(xre[...], xim[...])
    vre[: nb - 1] += alternate * vre[1:]
    vim[: nb - 1] += alternate * vim[1:]
    correlate()
    s4[:, 1] = (inverse() * (1.0 / math.sqrt(nb * n))).astype(BF16).reshape(nb, cb, n)
    start_exchange(3, s4, r4)
    sent(0, s1, r1)
    sent(1, s2, r2)
    lax.fori_loop(1, nchan, stat_sent, 0)
    sent(2, s3, r3)
    finish_exchange(3, s4, r4)
    ig_ref[...] = r4[:, 0].reshape(rows, n).astype(F32).T.astype(BF16)
    fg_ref[...] = r4[:, 1].reshape(rows, n).astype(F32).T
    sent(3, s4, r4)


def local(nb, nchan, inputs, gate, filter_taps, cotangent):
    n, local_chan = inputs.shape
    cb = local_chan // nb
    tables = [jnp.asarray(table) for table in dft_tables(n)]
    vmem = pl.BlockSpec(memory_space=pltpu.VMEM)
    one = pltpu.VMEM((nb, cb, n), BF16)
    two = pltpu.VMEM((nb, 2, cb, n), BF16)
    wide = pltpu.VMEM((nb, cb, n), F32)
    return pl.pallas_call(
        functools.partial(kernel, nb, nchan),
        out_shape=(
            jax.ShapeDtypeStruct((n, local_chan), BF16),
            jax.ShapeDtypeStruct((n, local_chan), BF16),
            jax.ShapeDtypeStruct((n, local_chan), BF16),
            jax.ShapeDtypeStruct((n, local_chan), F32),
        ),
        in_specs=[vmem] * 8,
        out_specs=(vmem,) * 4,
        scratch_shapes=[two, two, one, one, one, one, two, two, pltpu.VMEM((nchan, 2, n), F32)]
        + [wide] * 9
        + [
            pltpu.SemaphoreType.DMA((4, nb)),
            pltpu.SemaphoreType.DMA((4, nb)),
            pltpu.SemaphoreType.DMA((nchan,)),
            pltpu.SemaphoreType.DMA((nchan,)),
        ],
        compiler_params=pltpu.CompilerParams(collective_id=0, has_side_effects=True),
    )(inputs, gate, filter_taps, cotangent, *tables)


def solution(mesh):
    spec = P("ctx", "chan")
    body = functools.partial(local, mesh.shape["ctx"], mesh.shape["chan"])
    return jax.shard_map(
        body, mesh=mesh, in_specs=(spec,) * 4, out_specs=(spec,) * 4, check_vma=False
    )
```

```python
import functools
import math

import jax
import jax.numpy as jnp
import ml_dtypes
import numpy as np
from jax import lax
from jax.experimental import pallas as pl
from jax.experimental.pallas import tpu as pltpu
from jax.sharding import PartitionSpec as P

EPSILON = 1e-06
MESH = pl.DeviceIdType.MESH
BF16 = jnp.bfloat16
F32 = jnp.float32


def split_table(table):
    head = table.astype(ml_dtypes.bfloat16)
    rest = (table - head.astype(np.float64)).astype(ml_dtypes.bfloat16)
    return head, rest


def dft_tables(n):
    k = np.arange(n)
    t = np.arange(n)
    angles = np.mod(np.outer(t, k), 2 * n) * (math.pi / n)
    alternate = np.where(t % 2 == 0, 1.0, -1.0)
    sines = -np.sin(angles)
    sines[:, 0] = alternate
    fwd = np.concatenate([np.cos(angles), sines], axis=1)
    weights = np.where(k == 0, 1.0, 2.0) / (2 * n)
    inv = np.concatenate(
        [np.cos(angles) * weights[None, :], sines * weights[None, :]], axis=1
    ).T
    return split_table(fwd) + split_table(inv)


def each(indices, step):
    for k in indices:
        step(k, 0)


def kernel(
    nb, nchan,
    x_hbm, g_hbm, h_hbm, c_hbm, fhi_hbm, flo_hbm, ihi_hbm, ilo_hbm,
    out_ref, gg_ref, ig_ref, fg_ref,
    s1, r1, s2, r2, s3, r3, s4, r4, s5, r5, stats,
    xre, xim, kre, kre2, kim, vre, vim, qre, qim,
    x_ref, h_ref, g_ref, c_ref, fhi_ref, flo_ref, ihi_ref, ilo_ref,
    send_sems, recv_sems, stat_send, stat_recv, load_sems,
):
    me = lax.axis_index("ctx")
    mc = lax.axis_index("chan")
    n, local_chan = x_ref.shape
    cb = local_chan // nb
    rows = nb * cb
    channels = local_chan * nchan

    side = nb // 2
    half = lax.div(me, side)
    slot = lax.rem(me, side)
    peers = list(range(side, nb)) + list(range(1, side))

    def target(k):
        return lax.rem(half + k // side, 2) * side + lax.rem(slot + k, side)

    def origin(k):
        return lax.rem(half + k // side, 2) * side + lax.rem(slot + nb - k, side)

    barrier = pltpu.get_barrier_semaphore()

    def greet_ctx(k, _):
        pl.semaphore_signal(
            barrier, inc=1, device_id={"ctx": lax.rem(me + k, nb)}, device_id_type=MESH
        )
        return 0

    def greet_chan(k, _):
        pl.semaphore_signal(
            barrier, inc=1, device_id={"chan": lax.rem(mc + k, nchan)}, device_id_type=MESH
        )
        return 0

    each(range(1, nb), greet_ctx)
    each(range(1, nchan), greet_chan)

    pairs = (
        (x_hbm, x_ref), (h_hbm, h_ref), (g_hbm, g_ref), (c_hbm, c_ref),
        (fhi_hbm, fhi_ref), (flo_hbm, flo_ref), (ihi_hbm, ihi_ref), (ilo_hbm, ilo_ref),
    )
    loads = [pltpu.make_async_copy(a, b, load_sems.at[i]) for i, (a, b) in enumerate(pairs)]
    for load in loads:
        load.start()

    def turned(ref):
        return ref[...].astype(F32).T

    loads[0].wait()
    loads[1].wait()
    s1[:, 0] = turned(x_ref).astype(BF16).reshape(nb, cb, n)
    s1[:, 1] = turned(h_ref).astype(BF16).reshape(nb, cb, n)
    pl.semaphore_wait(barrier, nb + nchan - 2)

    def exchange(phase, src, dst, k):
        return pltpu.make_async_remote_copy(
            src_ref=src.at[target(k)],
            dst_ref=dst.at[me],
            send_sem=send_sems.at[phase, k],
            recv_sem=recv_sems.at[phase, k],
            device_id={"ctx": target(k)},
            device_id_type=MESH,
        )

    def start_exchange(phase, src, dst):
        def step(k, _):
            exchange(phase, src, dst, k).start()
            return 0

        each(peers, step)
        dst[me] = src[me]

    def arrived(phase, src, dst, k):
        return pltpu.make_async_remote_copy(
            src_ref=src.at[origin(k)],
            dst_ref=dst.at[origin(k)],
            send_sem=send_sems.at[phase, k],
            recv_sem=recv_sems.at[phase, k],
            device_id={"ctx": origin(k)},
            device_id_type=MESH,
        )

    def finish_exchange(phase, src, dst):
        def step(k, _):
            arrived(phase, src, dst, k).wait_recv()
            return 0

        each(peers, step)

    def sent(phase, src, dst):
        def step(k, _):
            exchange(phase, src, dst, k).wait_send()
            return 0

        each(peers, step)

    lane = lax.broadcasted_iota(jnp.int32, (1, 1, n), 2)
    alternate = jnp.where(lax.rem(lane, 2) == 0, 1.0, -1.0).astype(F32)
    first = lane == 0

    def spectrum(block):
        wide = jnp.dot(block, fhi_ref[...], preferred_element_type=F32) + jnp.dot(
            block, flo_ref[...], preferred_element_type=F32
        )
        return wide[:, :n].reshape(nb, cb, n), wide[:, n:].reshape(nb, cb, n)

    def inverse():
        def half(part, lo, hi):
            head = part.astype(BF16)
            rest = (part - head.astype(F32)).astype(BF16)
            return (
                jnp.dot(head, ihi_ref[lo:hi, :], preferred_element_type=F32)
                + jnp.dot(head, ilo_ref[lo:hi, :], preferred_element_type=F32)
                + jnp.dot(rest, ihi_ref[lo:hi, :], preferred_element_type=F32)
            )

        return half(qre[...].reshape(rows, n), 0, n) + half(qim[...].reshape(rows, n), n, 2 * n)

    def set_kernel(re, im):
        kre[...] = re
        kre2[...] = jnp.where(first, im, re)
        kim[...] = jnp.where(first, 0.0, im)

    def correlate():
        for d in range(nb):
            re, im = vre[d:], vim[d:]
            a, a2, b = kre[d : d + 1], kre2[d : d + 1], kim[d : d + 1]
            new_re = a * re + b * im
            new_im = a2 * im - b * re
            if d == 0:
                qre[...] = new_re
                qim[...] = new_im
            else:
                qre[: nb - d] += new_re
                qim[: nb - d] += new_im

    start_exchange(0, s1, r1)
    for load in loads[2:]:
        load.wait()
    gate = turned(g_ref)
    upstream = turned(c_ref)
    finish_exchange(0, s1, r1)

    x_re, x_im = spectrum(r1[:, 0].reshape(rows, n))
    xre[...] = x_re
    xim[...] = x_im
    h_re, h_im = spectrum(r1[:, 1].reshape(rows, n))
    zero = jnp.zeros((1, cb, n), F32)
    set_kernel(
        h_re + alternate * jnp.concatenate([zero, h_re[:-1]], axis=0),
        h_im + alternate * jnp.concatenate([zero, h_im[:-1]], axis=0),
    )
    for d in range(nb):
        re, im = xre[: nb - d], xim[: nb - d]
        a, a2, b = kre[d : d + 1], kre2[d : d + 1], kim[d : d + 1]
        new_re = a * re - b * im
        new_im = b * re + a2 * im
        if d == 0:
            qre[...] = new_re
            qim[...] = new_im
        else:
            qre[d:] += new_re
            qim[d:] += new_im
    s2[...] = inverse().astype(BF16).reshape(nb, cb, n)
    start_exchange(1, s2, r2)
    finish_exchange(1, s2, r2)

    convolved = r2[...].reshape(rows, n).astype(F32)
    mixed = gate * convolved
    stats[mc, 0:1, :] = jnp.sum(mixed * mixed, axis=0, keepdims=True)
    stats[mc, 1:2, :] = jnp.sum(upstream * mixed, axis=0, keepdims=True)

    def stat_copy(k):
        return pltpu.make_async_remote_copy(
            src_ref=stats.at[mc],
            dst_ref=stats.at[mc],
            send_sem=stat_send.at[k],
            recv_sem=stat_recv.at[k],
            device_id={"chan": lax.rem(mc + k, nchan)},
            device_id_type=MESH,
        )

    def stat_start(k, _):
        stat_copy(k).start()
        return 0

    def stat_wait(k, _):
        source = lax.rem(mc + nchan - k, nchan)
        pltpu.make_async_remote_copy(
            src_ref=stats.at[source],
            dst_ref=stats.at[source],
            send_sem=stat_send.at[k],
            recv_sem=stat_recv.at[k],
            device_id={"chan": source},
            device_id_type=MESH,
        ).wait_recv()
        return 0

    def stat_sent(k, _):
        stat_copy(k).wait_send()
        return 0

    each(range(1, nchan), stat_start)
    each(range(1, nchan), stat_wait)
    totals = jnp.sum(stats[...], axis=0)
    inv_rms = lax.rsqrt(totals[0:1] / channels + EPSILON)
    d_mixed = inv_rms * upstream - mixed * (inv_rms**3 * totals[1:2] / channels)
    s3[...] = (d_mixed * gate).astype(BF16).reshape(nb, cb, n)
    start_exchange(2, s3, r3)
    out_ref[...] = (mixed * inv_rms).astype(BF16)
    gg_ref[...] = (d_mixed * convolved).astype(BF16)
    finish_exchange(2, s3, r3)

    d_re, d_im = spectrum(r3[...].reshape(rows, n))
    vre[...] = d_re
    vim[...] = d_im
    correlate()
    s4[...] = inverse().astype(BF16).reshape(nb, cb, n)
    start_exchange(3, s4, r4)
    set_kernel(xre[...], xim[...])
    vre[: nb - 1] += alternate * vre[1:]
    vim[: nb - 1] += alternate * vim[1:]
    correlate()
    s5[...] = (inverse() * (1.0 / math.sqrt(nb * n))).astype(BF16).reshape(nb, cb, n)
    start_exchange(4, s5, r5)
    sent(0, s1, r1)
    sent(1, s2, r2)
    each(range(1, nchan), stat_sent)
    sent(2, s3, r3)
    finish_exchange(3, s4, r4)
    ig_ref[...] = r4[...].reshape(rows, n)
    finish_exchange(4, s5, r5)
    fg_ref[...] = r5[...].reshape(rows, n)
    sent(3, s4, r4)
    sent(4, s5, r5)


def finish(out_t, gg_t, ig_t, fg_t, out_ref, gg_ref, ig_ref, fg_ref):
    out_ref[...] = out_t[...].astype(F32).T.astype(BF16)
    gg_ref[...] = gg_t[...].astype(F32).T.astype(BF16)
    ig_ref[...] = ig_t[...].astype(F32).T.astype(BF16)
    fg_ref[...] = fg_t[...].astype(F32).T


def local(nb, nchan, inputs, gate, filter_taps, cotangent):
    n, local_chan = inputs.shape
    cb = local_chan // nb
    tables = [jnp.asarray(table) for table in dft_tables(n)]
    vmem = pl.BlockSpec(memory_space=pltpu.VMEM)
    one = pltpu.VMEM((nb, cb, n), BF16)
    two = pltpu.VMEM((nb, 2, cb, n), BF16)
    wide = pltpu.VMEM((nb, cb, n), F32)
    turned = pl.pallas_call(
        functools.partial(kernel, nb, nchan),
        out_shape=(jax.ShapeDtypeStruct((local_chan, n), BF16),) * 4,
        in_specs=[pl.BlockSpec(memory_space=pl.ANY)] * 8,
        out_specs=(vmem,) * 4,
        scratch_shapes=[two, two, one, one, one, one, one, one, one, one, pltpu.VMEM((nchan, 2, n), F32)]
        + [wide] * 9
        + [pltpu.VMEM((n, local_chan), BF16)] * 4
        + [pltpu.VMEM((n, 2 * n), BF16)] * 2
        + [pltpu.VMEM((2 * n, n), BF16)] * 2
        + [
            pltpu.SemaphoreType.DMA((5, nb)),
            pltpu.SemaphoreType.DMA((5, nb)),
            pltpu.SemaphoreType.DMA((nchan,)),
            pltpu.SemaphoreType.DMA((nchan,)),
            pltpu.SemaphoreType.DMA((8,)),
        ],
        compiler_params=pltpu.CompilerParams(collective_id=0, has_side_effects=True),
    )(inputs, gate, filter_taps, cotangent, *tables)
    return pl.pallas_call(
        finish,
        out_shape=(
            jax.ShapeDtypeStruct((n, local_chan), BF16),
            jax.ShapeDtypeStruct((n, local_chan), BF16),
            jax.ShapeDtypeStruct((n, local_chan), BF16),
            jax.ShapeDtypeStruct((n, local_chan), F32),
        ),
        in_specs=[vmem] * 4,
        out_specs=(vmem,) * 4,
    )(*turned)


def solution(mesh):
    spec = P("ctx", "chan")
    body = functools.partial(local, mesh.shape["ctx"], mesh.shape["chan"])
    return jax.shard_map(
        body, mesh=mesh, in_specs=(spec,) * 4, out_specs=(spec,) * 4, check_vma=False
    )
```

```python
import functools
import math

import jax
import jax.numpy as jnp
import ml_dtypes
import numpy as np
from jax import lax
from jax.experimental import pallas as pl
from jax.experimental.pallas import tpu as pltpu
from jax.sharding import PartitionSpec as P

EPSILON = 1e-06
MESH = pl.DeviceIdType.MESH
BF16 = jnp.bfloat16
F32 = jnp.float32


def split_table(table):
    head = table.astype(ml_dtypes.bfloat16)
    rest = (table - head.astype(np.float64)).astype(ml_dtypes.bfloat16)
    return head, rest


def dft_tables(n):
    k = np.arange(n)
    t = np.arange(n)
    angles = np.mod(np.outer(t, k), 2 * n) * (math.pi / n)
    alternate = np.where(t % 2 == 0, 1.0, -1.0)
    sines = -np.sin(angles)
    sines[:, 0] = alternate
    fwd = np.concatenate([np.cos(angles), sines], axis=1)
    weights = np.where(k == 0, 1.0, 2.0) / (2 * n)
    inv = np.concatenate(
        [np.cos(angles) * weights[None, :], sines * weights[None, :]], axis=1
    ).T
    return split_table(fwd) + split_table(inv)


def each(indices, step):
    for k in indices:
        step(k, 0)


def kernel(
    nb, nchan,
    x_hbm, g_hbm, h_hbm, c_hbm, fhi_hbm, flo_hbm, ihi_hbm, ilo_hbm,
    out_ref, gg_ref, ig_ref, fg_ref,
    s1, r1, s2, r2, s3, r3, s4, r4, s5, r5, stats,
    xre, xim, kre, kre2, kim, vre, vim, qre, qim,
    x_ref, h_ref, g_ref, c_ref, fhi_ref, flo_ref, ihi_ref, ilo_ref,
    send_sems, recv_sems, stat_send, stat_recv, load_sems,
):
    me = lax.axis_index("ctx")
    mc = lax.axis_index("chan")
    n, local_chan = x_ref.shape
    cb = local_chan // nb
    rows = nb * cb
    channels = local_chan * nchan

    side = nb // 2
    half = lax.div(me, side)
    slot = lax.rem(me, side)
    peers = list(range(side, nb)) + list(range(1, side))

    def target(k):
        return lax.rem(half + k // side, 2) * side + lax.rem(slot + k, side)

    def origin(k):
        return lax.rem(half + k // side, 2) * side + lax.rem(slot + nb - k, side)

    barrier = pltpu.get_barrier_semaphore()

    def greet_ctx(k, _):
        pl.semaphore_signal(
            barrier, inc=1, device_id={"ctx": lax.rem(me + k, nb)}, device_id_type=MESH
        )
        return 0

    def greet_chan(k, _):
        pl.semaphore_signal(
            barrier, inc=1, device_id={"chan": lax.rem(mc + k, nchan)}, device_id_type=MESH
        )
        return 0

    each(range(1, nb), greet_ctx)
    each(range(1, nchan), greet_chan)

    pairs = (
        (x_hbm, x_ref), (h_hbm, h_ref), (g_hbm, g_ref), (c_hbm, c_ref),
        (fhi_hbm, fhi_ref), (flo_hbm, flo_ref), (ihi_hbm, ihi_ref), (ilo_hbm, ilo_ref),
    )
    loads = [pltpu.make_async_copy(a, b, load_sems.at[i]) for i, (a, b) in enumerate(pairs)]
    for load in loads:
        load.start()

    def turned(ref):
        return ref[...].astype(F32).T

    loads[0].wait()
    loads[1].wait()
    s1[:, 0] = turned(x_ref).astype(BF16).reshape(nb, cb, n)
    s1[:, 1] = turned(h_ref).astype(BF16).reshape(nb, cb, n)
    pl.semaphore_wait(barrier, nb + nchan - 2)

    def exchange(phase, src, dst, k):
        return pltpu.make_async_remote_copy(
            src_ref=src.at[target(k)],
            dst_ref=dst.at[me],
            send_sem=send_sems.at[phase, k],
            recv_sem=recv_sems.at[phase, k],
            device_id={"ctx": target(k)},
            device_id_type=MESH,
        )

    def start_exchange(phase, src, dst):
        def step(k, _):
            exchange(phase, src, dst, k).start()
            return 0

        each(peers, step)
        dst[me] = src[me]

    def arrived(phase, src, dst, k):
        return pltpu.make_async_remote_copy(
            src_ref=src.at[origin(k)],
            dst_ref=dst.at[origin(k)],
            send_sem=send_sems.at[phase, k],
            recv_sem=recv_sems.at[phase, k],
            device_id={"ctx": origin(k)},
            device_id_type=MESH,
        )

    def finish_exchange(phase, src, dst):
        def step(k, _):
            arrived(phase, src, dst, k).wait_recv()
            return 0

        each(peers, step)

    def sent(phase, src, dst):
        def step(k, _):
            exchange(phase, src, dst, k).wait_send()
            return 0

        each(peers, step)

    lane = lax.broadcasted_iota(jnp.int32, (1, 1, n), 2)
    alternate = jnp.where(lax.rem(lane, 2) == 0, 1.0, -1.0).astype(F32)
    first = lane == 0

    def spectrum(block):
        wide = jnp.dot(block, fhi_ref[...], preferred_element_type=F32) + jnp.dot(
            block, flo_ref[...], preferred_element_type=F32
        )
        return wide[:, :n].reshape(nb, cb, n), wide[:, n:].reshape(nb, cb, n)

    def inverse():
        def half(part, lo, hi):
            head = part.astype(BF16)
            rest = (part - head.astype(F32)).astype(BF16)
            return (
                jnp.dot(head, ihi_ref[lo:hi, :], preferred_element_type=F32)
                + jnp.dot(head, ilo_ref[lo:hi, :], preferred_element_type=F32)
                + jnp.dot(rest, ihi_ref[lo:hi, :], preferred_element_type=F32)
            )

        return half(qre[...].reshape(rows, n), 0, n) + half(qim[...].reshape(rows, n), n, 2 * n)

    def set_kernel(re, im):
        kre[...] = re
        kre2[...] = jnp.where(first, im, re)
        kim[...] = jnp.where(first, 0.0, im)

    def correlate():
        for d in range(nb):
            re, im = vre[d:], vim[d:]
            a, a2, b = kre[d : d + 1], kre2[d : d + 1], kim[d : d + 1]
            new_re = a * re + b * im
            new_im = a2 * im - b * re
            if d == 0:
                qre[...] = new_re
                qim[...] = new_im
            else:
                qre[: nb - d] += new_re
                qim[: nb - d] += new_im

    start_exchange(0, s1, r1)
    for load in loads[2:]:
        load.wait()
    gate = turned(g_ref)
    upstream = turned(c_ref)
    finish_exchange(0, s1, r1)

    x_re, x_im = spectrum(r1[:, 0].reshape(rows, n))
    xre[...] = x_re
    xim[...] = x_im
    h_re, h_im = spectrum(r1[:, 1].reshape(rows, n))
    zero = jnp.zeros((1, cb, n), F32)
    set_kernel(
        h_re + alternate * jnp.concatenate([zero, h_re[:-1]], axis=0),
        h_im + alternate * jnp.concatenate([zero, h_im[:-1]], axis=0),
    )
    for d in range(nb):
        re, im = xre[: nb - d], xim[: nb - d]
        a, a2, b = kre[d : d + 1], kre2[d : d + 1], kim[d : d + 1]
        new_re = a * re - b * im
        new_im = b * re + a2 * im
        if d == 0:
            qre[...] = new_re
            qim[...] = new_im
        else:
            qre[d:] += new_re
            qim[d:] += new_im
    s2[...] = inverse().astype(BF16).reshape(nb, cb, n)
    start_exchange(1, s2, r2)
    finish_exchange(1, s2, r2)

    convolved = r2[...].reshape(rows, n).astype(F32)
    mixed = gate * convolved
    stats[mc, 0:1, :] = jnp.sum(mixed * mixed, axis=0, keepdims=True)
    stats[mc, 1:2, :] = jnp.sum(upstream * mixed, axis=0, keepdims=True)

    def stat_copy(k):
        return pltpu.make_async_remote_copy(
            src_ref=stats.at[mc],
            dst_ref=stats.at[mc],
            send_sem=stat_send.at[k],
            recv_sem=stat_recv.at[k],
            device_id={"chan": lax.rem(mc + k, nchan)},
            device_id_type=MESH,
        )

    def stat_start(k, _):
        stat_copy(k).start()
        return 0

    def stat_wait(k, _):
        source = lax.rem(mc + nchan - k, nchan)
        pltpu.make_async_remote_copy(
            src_ref=stats.at[source],
            dst_ref=stats.at[source],
            send_sem=stat_send.at[k],
            recv_sem=stat_recv.at[k],
            device_id={"chan": source},
            device_id_type=MESH,
        ).wait_recv()
        return 0

    def stat_sent(k, _):
        stat_copy(k).wait_send()
        return 0

    each(sorted(range(1, nchan), key=lambda k: abs(k % 8 - 4)), stat_start)
    each(range(1, nchan), stat_wait)
    totals = jnp.sum(stats[...], axis=0)
    inv_rms = lax.rsqrt(totals[0:1] / channels + EPSILON)
    d_mixed = inv_rms * upstream - mixed * (inv_rms**3 * totals[1:2] / channels)
    s3[...] = (d_mixed * gate).astype(BF16).reshape(nb, cb, n)
    start_exchange(2, s3, r3)
    out_ref[...] = (mixed * inv_rms).astype(BF16)
    gg_ref[...] = (d_mixed * convolved).astype(BF16)
    finish_exchange(2, s3, r3)

    d_re, d_im = spectrum(r3[...].reshape(rows, n))
    vre[...] = d_re
    vim[...] = d_im
    correlate()
    s4[...] = inverse().astype(BF16).reshape(nb, cb, n)
    start_exchange(3, s4, r4)
    set_kernel(xre[...], xim[...])
    vre[: nb - 1] += alternate * vre[1:]
    vim[: nb - 1] += alternate * vim[1:]
    correlate()
    s5[...] = (inverse() * (1.0 / math.sqrt(nb * n))).astype(BF16).reshape(nb, cb, n)
    start_exchange(4, s5, r5)
    sent(0, s1, r1)
    sent(1, s2, r2)
    each(range(1, nchan), stat_sent)
    sent(2, s3, r3)
    finish_exchange(3, s4, r4)
    ig_ref[...] = r4[...].reshape(rows, n)
    finish_exchange(4, s5, r5)
    fg_ref[...] = r5[...].reshape(rows, n)
    sent(3, s4, r4)
    sent(4, s5, r5)


def finish(out_t, gg_t, ig_t, fg_t, out_ref, gg_ref, ig_ref, fg_ref):
    out_ref[...] = out_t[...].astype(F32).T.astype(BF16)
    gg_ref[...] = gg_t[...].astype(F32).T.astype(BF16)
    ig_ref[...] = ig_t[...].astype(F32).T.astype(BF16)
    fg_ref[...] = fg_t[...].astype(F32).T


def local(nb, nchan, inputs, gate, filter_taps, cotangent):
    n, local_chan = inputs.shape
    cb = local_chan // nb
    tables = [jnp.asarray(table) for table in dft_tables(n)]
    vmem = pl.BlockSpec(memory_space=pltpu.VMEM)
    one = pltpu.VMEM((nb, cb, n), BF16)
    two = pltpu.VMEM((nb, 2, cb, n), BF16)
    wide = pltpu.VMEM((nb, cb, n), F32)
    turned = pl.pallas_call(
        functools.partial(kernel, nb, nchan),
        out_shape=(jax.ShapeDtypeStruct((local_chan, n), BF16),) * 4,
        in_specs=[pl.BlockSpec(memory_space=pl.ANY)] * 8,
        out_specs=(vmem,) * 4,
        scratch_shapes=[two, two, one, one, one, one, one, one, one, one, pltpu.VMEM((nchan, 2, n), F32)]
        + [wide] * 9
        + [pltpu.VMEM((n, local_chan), BF16)] * 4
        + [pltpu.VMEM((n, 2 * n), BF16)] * 2
        + [pltpu.VMEM((2 * n, n), BF16)] * 2
        + [
            pltpu.SemaphoreType.DMA((5, nb)),
            pltpu.SemaphoreType.DMA((5, nb)),
            pltpu.SemaphoreType.DMA((nchan,)),
            pltpu.SemaphoreType.DMA((nchan,)),
            pltpu.SemaphoreType.DMA((8,)),
        ],
        compiler_params=pltpu.CompilerParams(collective_id=0, has_side_effects=True),
    )(inputs, gate, filter_taps, cotangent, *tables)
    return pl.pallas_call(
        finish,
        out_shape=(
            jax.ShapeDtypeStruct((n, local_chan), BF16),
            jax.ShapeDtypeStruct((n, local_chan), BF16),
            jax.ShapeDtypeStruct((n, local_chan), BF16),
            jax.ShapeDtypeStruct((n, local_chan), F32),
        ),
        in_specs=[vmem] * 4,
        out_specs=(vmem,) * 4,
    )(*turned)


def solution(mesh):
    spec = P("ctx", "chan")
    body = functools.partial(local, mesh.shape["ctx"], mesh.shape["chan"])
    return jax.shard_map(
        body, mesh=mesh, in_specs=(spec,) * 4, out_specs=(spec,) * 4, check_vma=False
    )
```
